32 devices in a mesh: replica: 8 (over y, x, core), tensor: 4 (over z).
Axes of the slice: x: 2, y: 2, z: 4, core: 2. Of those that a mesh axis runs over, the one named last changes fastest.
Arguments:
- weights: bfloat16 [8, 8192, 2048], P('replica', 'tensor'), may hold values from -6 to 6
- hidden: bfloat16 [8, 512, 8192], P('replica', None, 'tensor'), may hold values from -6 to 6
- out_grad: bfloat16 [8, 512, 2048], P('replica', None, 'tensor'), may hold values from -0.375 to 0.375
- factor_start: bfloat16 [2, 64, 8192], P(None, None, 'tensor'), may hold values from -6 to 6
- matching: int32 [2], replicated, may hold values from 1 to 7, as said below
Outputs:
- new_weights: bfloat16 [8, 8192, 2048], P('replica', 'tensor')
The draws below stay inside these ranges and needn't reach their ends.
Inputs may be any that keep to these rules, and one draw needn't show every extreme that they name: In step t replica i is matched with replica i XOR matching[t]; in one of the steps matching equals 7.
All inputs are finite; a program needn't handle non-finite values.
Results may differ from the reference program's by a relative error of at most 0.014.
Values may be sent and summed in bfloat16 or wider, within the bound.
No kernel may reach another device: no remote copies, remote signals or barrier semaphores. Data moves between devices by JAX's collectives and lax.ppermute only.
A program may use at most 128 MiB of HBM per device.

```python
import jax
import jax.numpy as jnp
from jax import lax

D = 2048
FF = 8192
R = 64
STEPS = 2
TOK = 256
N_REPLICA = 8


def draw_matching(key, part):
    first_key, second_key = jax.random.split(jax.random.fold_in(key, 17))
    others = jax.random.randint(first_key, (STEPS,), 1, N_REPLICA - 1)
    chosen = jax.random.randint(second_key, (), 0, STEPS)
    return jnp.where(jnp.arange(STEPS) == chosen, N_REPLICA - 1, others).astype(jnp.int32)


def levels(key, dims, cuts, smallest, largest):
    loudness = 1.0
    for axis_at, blocks in cuts:
        heights = jax.random.uniform(jax.random.fold_in(jax.random.fold_in(key, 6), axis_at), (blocks,), jnp.float32, smallest / len(cuts), largest / len(cuts))
        loudness = loudness * jnp.repeat(jnp.exp(heights), dims[axis_at] // blocks).reshape((-1,) + (1,) * (len(dims) - 1 - axis_at))
    return loudness


def bell_draw(key, extent, width, bound, shards=(), held_as=jnp.bfloat16):
    loudness = levels(key, extent, shards, -0.22, 0.18) if shards else 1.0
    values = jax.random.normal(key, extent, jnp.float32) * width * loudness
    return jnp.minimum(jnp.maximum(values, -bound), bound).astype(held_as)


def setup_inputs(seed: int = 0) -> dict:
    splits = jax.random.split(jax.random.key(seed), 6)
    weights = bell_draw(splits[0], (N_REPLICA, FF, D), 1.0, 6.0, ((0, 8), (1, 4)))
    hidden = bell_draw(splits[1], (N_REPLICA, STEPS * TOK, FF), 1.0, 6.0, ((0, 8), (2, 4)))
    out_grad = bell_draw(splits[2], (N_REPLICA, STEPS * TOK, D), (1.0 / TOK ** 0.5), 0.375, ((0, 8), (2, 4)))
    factor_start = bell_draw(splits[3], (STEPS, R, FF), 1.0, 6.0, ((2, 4),))
    matching = draw_matching(jax.random.fold_in(splits[5], 71), 0)
    return {"weights": weights, "hidden": hidden, "out_grad": out_grad, "factor_start": factor_start, "matching": matching}


learn_rate = 0.1
momentum_decay = 0.9

def reference(weights, hidden, out_grad, factor_start, matching):
    replica_ids = jnp.arange(N_REPLICA, dtype=jnp.int32)
    current = weights
    momentum = None
    for step_index in range(STEPS):
        hidden_step = hidden[:, step_index * TOK:(step_index + 1) * TOK]
        grads_step = out_grad[:, step_index * TOK:(step_index + 1) * TOK]
        keep_state = step_index + 1 < STEPS
        has_earlier = step_index > 0

        def advance(operands):
            gradient = jnp.dot(operands[0].T.astype(jnp.float32), operands[1].astype(jnp.float32), preferred_element_type=jnp.float32)
            if has_earlier:
                gradient = momentum_decay * operands[3] + gradient
            renewed = (operands[2].astype(jnp.float32) - learn_rate * gradient).astype(jnp.bfloat16)
            if keep_state:
                return (gradient, renewed)
            return renewed
        operand_list = (hidden_step, grads_step, current)
        if has_earlier:
            operand_list = operand_list + (momentum,)
        if keep_state:
            momentum, updated = lax.map(advance, operand_list)
        else:
            updated = lax.map(advance, operand_list)
        start_factor = factor_start[step_index]

        def left_product(weight_rows):
            return jnp.dot(start_factor.astype(jnp.float32), weight_rows.astype(jnp.float32), preferred_element_type=jnp.float32)
        left_all = lax.map(left_product, updated)
        partner = jnp.bitwise_xor(replica_ids, matching[step_index]).astype(jnp.int32)
        left_diff = left_all - left_all[partner]
        gram = jnp.einsum('irk,isk->irs', left_diff, left_diff, precision=lax.Precision.HIGHEST)
        lower_factor = jnp.linalg.cholesky(gram)
        ortho = lax.linalg.triangular_solve(lower_factor, left_diff, left_side=True, lower=True)
        ortho_bf = ortho.astype(jnp.bfloat16)

        def right_product(operands):
            return jnp.dot(operands[0].astype(jnp.float32), operands[1].T.astype(jnp.float32), preferred_element_type=jnp.float32)
        right_all = lax.map(right_product, (ortho_bf, updated))
        right_diff = (right_all - right_all[partner]).astype(jnp.bfloat16)

        def move_half(operands):
            change = jnp.dot(operands[1].T.astype(jnp.float32), operands[2].astype(jnp.float32), preferred_element_type=jnp.float32)
            return (operands[0].astype(jnp.float32) - 0.5 * change).astype(jnp.bfloat16)
        current = lax.map(move_half, (updated, right_diff, ortho_bf))
    return current
```

```python
import functools

import jax
import jax.numpy as jnp
from jax import lax
from jax.experimental import pallas as pl
from jax.experimental.pallas import tpu as pltpu
from jax.sharding import PartitionSpec as P

learn_rate = 0.1
momentum_decay = 0.9
older_share = learn_rate * (1.0 + momentum_decay)
bf16 = jnp.bfloat16
f32 = jnp.float32

VMEM = pl.BlockSpec(memory_space=pltpu.VMEM)
SMEM = pl.BlockSpec(memory_space=pltpu.SMEM)


def dot(a, b, contract, precision=None):
    return lax.dot_general(
        a, b, (((contract[0],), (contract[1],)), ((), ())),
        precision=precision, preferred_element_type=f32,
    )


def exact(a, b, contract):
    return dot(a, b, contract, lax.Precision.HIGHEST)


def columns_of(place, width):
    return pl.ds(pl.multiple_of(place * width, width), width)


def project_kernel(count, rank, tokens, me_ref, f_ref, h_ref, w_ref, *refs):
    messages, seen = refs[:count], refs[count]
    step = pl.program_id(0)
    span = w_ref.shape[1]

    @pl.when(step == 0)
    def _():
        both = dot(f_ref[...], h_ref[...], (1, 1)).astype(bf16)
        seen[:, :tokens] = both[:rank, :tokens]
        seen[:, tokens : 2 * tokens] = both[rank:, :tokens]
        seen[:, 2 * tokens :] = both[rank:, tokens:]

    part = dot(f_ref[...], w_ref[...], (1, 0)).astype(bf16)
    for k in range(count):
        @pl.when(step == k)
        def _(k=k):
            messages[k][:, :span] = part[:rank]
            messages[k][:, span : 2 * span] = part[rank:]
            messages[k][:, 2 * span :] = seen[...]


def project(me, factors, h, w, count, rank, tokens):
    width, depth = w.shape
    span = depth // count
    length = 2 * span + 3 * tokens
    return pl.pallas_call(
        functools.partial(project_kernel, count, rank, tokens),
        grid_spec=pltpu.PrefetchScalarGridSpec(
            num_scalar_prefetch=1,
            grid=(count,),
            in_specs=[
                pl.BlockSpec(factors.shape, lambda k, me: (0, 0)),
                pl.BlockSpec(h.shape, lambda k, me: (0, 0)),
                pl.BlockSpec((width, span), lambda k, me: (0, lax.rem(me[0] + k, count))),
            ],
            out_specs=[pl.BlockSpec((rank, length), lambda k, me: (0, 0))] * count,
            scratch_shapes=[pltpu.VMEM((rank, 3 * tokens), bf16)],
        ),
        out_shape=[jax.ShapeDtypeStruct((rank, length), bf16)] * count,
        name="project",
    )(me, factors, h, w)


def left_kernel(count, tokens, g_ref, *refs):
    messages, (mine, left) = refs[:count], refs[count:]
    span = g_ref.shape[1]
    total = messages[0][...].astype(f32)
    for k in range(1, count):
        total = total + messages[k][...].astype(f32)
    seen = total[:, 2 * span :].astype(bf16)
    older = dot(seen[:, tokens : 2 * tokens], g_ref[:tokens, :], (1, 0))
    mine[:, :span] = (
        total[:, :span] - learn_rate * dot(seen[:, :tokens], g_ref[:tokens, :], (1, 0))
    ).astype(bf16)
    later = total[:, span : 2 * span] - learn_rate * older
    mine[:, span:] = later.astype(bf16)
    left[...] = later - learn_rate * (
        momentum_decay * older + dot(seen[:, 2 * tokens :], g_ref[tokens:, :], (1, 0))
    )


def left_products(g, messages, tokens):
    rank, span = messages[0].shape[0], g.shape[1]
    return pl.pallas_call(
        functools.partial(left_kernel, len(messages), tokens),
        out_shape=[
            jax.ShapeDtypeStruct((rank, 2 * span), bf16),
            jax.ShapeDtypeStruct((rank, span), f32),
        ],
        in_specs=[VMEM] * (1 + len(messages)),
        out_specs=[VMEM] * 2,
        name="left",
    )(g, *messages)


def differ_kernel(mine, other, out):
    rank, length = mine.shape
    span = length // 2
    diff = (mine[:, :span].astype(f32) - other[:, :span].astype(f32)).astype(bf16)
    both = (mine[:, span:].astype(f32) + other[:, span:].astype(f32)).astype(bf16)
    out[:, :span] = diff
    out[:, span:] = dot(both, diff, (1, 1)).astype(bf16)


def differ(mine, other):
    rank, length = mine.shape
    return pl.pallas_call(
        differ_kernel,
        out_shape=jax.ShapeDtypeStruct((rank, length // 2 + rank), bf16),
        in_specs=[VMEM] * 2,
        out_specs=VMEM,
        name="differ",
    )(mine, other)


def inverse_factor(gram):
    size = gram.shape[0]
    work = gram
    rows = lax.broadcasted_iota(jnp.int32, (size, size), 0)
    columns = lax.broadcasted_iota(jnp.int32, (size, size), 1)
    scale = jnp.ones((size, size), f32)
    for k in range(size):
        pivot_row = work[k : k + 1, :]
        pivot = work[k : k + 1, k : k + 1]
        row = jnp.where(columns[:1] == k, 1.0, pivot_row) / pivot
        ratio = jnp.where(rows > k, work[:, k : k + 1], 0.0)
        kept = jnp.where((columns == k) & (rows > k), 0.0, work)
        work = kept - ratio * row
        scale = jnp.where(rows == k, pivot, scale)
    lower = jnp.where(rows > columns, work, jnp.where(rows == columns, 1.0, 0.0))
    return lower * lax.rsqrt(scale)


def ortho_first_kernel(count, me_ref, left_ref, *refs):
    messages, (ortho, out, whole) = refs[:count], refs[count:]
    rank, span = left_ref.shape
    edge = jnp.zeros((rank, rank), f32)
    for k in range(count):
        place = lax.rem(me_ref[0] + count - k, count)
        whole[:, columns_of(place, span)] = messages[k][:, :span]
        edge = edge + messages[k][:, span:].astype(f32)
    inverse = inverse_factor(dot(whole[...], whole[...], (1, 1)))
    near = exact(inverse, messages[0][:, :span].astype(f32), (1, 0)).astype(bf16)
    turned = exact(edge, inverse, (1, 1)).astype(bf16)
    out[...] = (left_ref[...] - 0.5 * dot(turned, near, (1, 0))).astype(bf16)
    ortho[...] = exact(inverse, whole[...].astype(f32), (1, 0)).astype(bf16)


def ortho_first(me, left, messages):
    count = len(messages)
    rank, span = left.shape
    return pl.pallas_call(
        functools.partial(ortho_first_kernel, count),
        out_shape=[
            jax.ShapeDtypeStruct((rank, span * count), bf16),
            jax.ShapeDtypeStruct((rank, span), bf16),
        ],
        in_specs=[SMEM] + [VMEM] * (1 + count),
        out_specs=[VMEM] * 2,
        scratch_shapes=[pltpu.VMEM((rank, span * count), bf16)],
        name="ortho_first",
    )(me, left, *messages)


def ortho_second_kernel(count, me_ref, *refs):
    messages, (ortho, whole) = refs[:count], refs[count:]
    span = messages[0].shape[1]
    for k in range(count):
        place = lax.rem(me_ref[0] + count - k, count)
        whole[:, columns_of(place, span)] = messages[k][...]
    inverse = inverse_factor(dot(whole[...], whole[...], (1, 1)))
    ortho[...] = exact(inverse, whole[...].astype(f32), (1, 0)).astype(bf16)


def ortho_second(me, messages):
    count = len(messages)
    rank, span = messages[0].shape
    return pl.pallas_call(
        functools.partial(ortho_second_kernel, count),
        out_shape=jax.ShapeDtypeStruct((rank, span * count), bf16),
        in_specs=[SMEM] + [VMEM] * count,
        out_specs=VMEM,
        scratch_shapes=[pltpu.VMEM((rank, span * count), bf16)],
        name="ortho_second",
    )(me, *messages)


def block_of(width):
    return min(width, 256)


def right_first_kernel(count, tokens, me_ref, ortho, h_ref, w_ref, *refs):
    grads, (out, seen) = refs[:count], refs[count:]
    span = grads[0].shape[1]

    @pl.when(pl.program_id(0) == 0)
    def _():
        total = jnp.zeros(seen.shape, f32)
        for k in range(count):
            place = lax.rem(me_ref[0] + count - k, count)
            total = total + dot(ortho[:, columns_of(place, span)], grads[k][...], (1, 1))
        seen[...] = (learn_rate * total).astype(bf16)

    out[...] = (
        dot(ortho[...], w_ref[...], (1, 1)) - dot(seen[...], h_ref[...], (1, 0))
    ).astype(bf16)


def right_first(me, ortho, h, w, grads, tokens):
    width, depth = w.shape
    rank = ortho.shape[0]
    count = len(grads)
    span = grads[0].shape[1]
    size = block_of(width)
    return pl.pallas_call(
        functools.partial(right_first_kernel, count, tokens),
        grid_spec=pltpu.PrefetchScalarGridSpec(
            num_scalar_prefetch=1,
            grid=(width // size,),
            in_specs=[
                pl.BlockSpec((rank, depth), lambda i, me: (0, 0)),
                pl.BlockSpec((tokens, size), lambda i, me: (0, i)),
                pl.BlockSpec((size, depth), lambda i, me: (i, 0)),
            ]
            + [pl.BlockSpec((tokens, span), lambda i, me: (0, 0))] * count,
            out_specs=pl.BlockSpec((rank, size), lambda i, me: (0, i)),
            scratch_shapes=[pltpu.VMEM((rank, tokens), bf16)],
        ),
        out_shape=jax.ShapeDtypeStruct((rank, width), bf16),
        name="right_first",
    )(me, ortho, h, w, *grads)


def right_second_kernel(count, tokens, me_ref, ortho, before, h_ref, w_ref, mine, other, *refs):
    grads, (out, seen, turned) = refs[:count], refs[count:]
    span = grads[0].shape[1]

    @pl.when(pl.program_id(0) == 0)
    def _():
        total = jnp.zeros(seen.shape, f32)
        for k in range(count):
            place = lax.rem(me_ref[0] + count - k, count)
            total = total + dot(ortho[:, columns_of(place, span)], grads[k][...], (1, 1))
        seen[:, :tokens] = (older_share * total[:, :tokens]).astype(bf16)
        seen[:, tokens:] = (learn_rate * total[:, tokens:]).astype(bf16)
        turned[...] = (0.5 * dot(ortho[...], before[...], (1, 1))).astype(bf16)

    turn = (mine[...].astype(f32) - other[...].astype(f32)).astype(bf16)
    out[...] = (
        dot(ortho[...], w_ref[...], (1, 1))
        - dot(seen[...], h_ref[...], (1, 0))
        - dot(turned[...], turn, (1, 0))
    ).astype(bf16)


def right_second(me, ortho, before, h, w, mine, other, grads, tokens):
    width, depth = w.shape
    rank = ortho.shape[0]
    count = len(grads)
    span = grads[0].shape[1]
    size = block_of(width)
    return pl.pallas_call(
        functools.partial(right_second_kernel, count, tokens),
        grid_spec=pltpu.PrefetchScalarGridSpec(
            num_scalar_prefetch=1,
            grid=(width // size,),
            in_specs=[
                pl.BlockSpec((rank, depth), lambda i, me: (0, 0)),
                pl.BlockSpec((rank, depth), lambda i, me: (0, 0)),
                pl.BlockSpec((2 * tokens, size), lambda i, me: (0, i)),
                pl.BlockSpec((size, depth), lambda i, me: (i, 0)),
                pl.BlockSpec((rank, size), lambda i, me: (0, i)),
                pl.BlockSpec((rank, size), lambda i, me: (0, i)),
            ]
            + [pl.BlockSpec((2 * tokens, span), lambda i, me: (0, 0))] * count,
            out_specs=pl.BlockSpec((rank, size), lambda i, me: (0, i)),
            scratch_shapes=[pltpu.VMEM((rank, 2 * tokens), bf16), pltpu.VMEM((rank, rank), bf16)],
        ),
        out_shape=jax.ShapeDtypeStruct((rank, width), bf16),
        name="right_second",
    )(me, ortho, before, h, w, mine, other, *grads)


def move_kernel(count, tokens, me_ref, first, second, h_ref, w_ref, a0, b0, a1, b1, *refs):
    grads, (out,) = refs[:count], refs[count:]
    span = grads[0].shape[1]
    share = h_ref[...].astype(f32)
    rows = lax.broadcasted_iota(jnp.int32, share.shape, 0)
    share = (share * jnp.where(rows < tokens, older_share, learn_rate)).astype(bf16)
    turn0 = (0.5 * (a0[...].astype(f32) - b0[...].astype(f32))).astype(bf16)
    turn1 = (0.5 * (a1[...].astype(f32) - b1[...].astype(f32))).astype(bf16)
    turn = jnp.concatenate([turn0, turn1], 0)
    for k in range(count):
        at = columns_of(lax.rem(me_ref[0] + count - k, count), span)
        ortho = jnp.concatenate([first[:, at], second[:, at]], 0)
        out[:, at] = (
            w_ref[:, at].astype(f32) - dot(share, grads[k][...], (0, 0)) - dot(turn, ortho, (0, 0))
        ).astype(bf16)


def move(me, first, second, h, w, pairs, grads, tokens):
    width, depth = w.shape
    rank = first.shape[0]
    count = len(grads)
    span = grads[0].shape[1]
    size = block_of(width)
    return pl.pallas_call(
        functools.partial(move_kernel, count, tokens),
        grid_spec=pltpu.PrefetchScalarGridSpec(
            num_scalar_prefetch=1,
            grid=(width // size,),
            in_specs=[
                pl.BlockSpec((rank, depth), lambda i, me: (0, 0)),
                pl.BlockSpec((rank, depth), lambda i, me: (0, 0)),
                pl.BlockSpec((2 * tokens, size), lambda i, me: (0, i)),
                pl.BlockSpec((size, depth), lambda i, me: (i, 0)),
            ]
            + [pl.BlockSpec((rank, size), lambda i, me: (0, i))] * 4
            + [pl.BlockSpec((2 * tokens, span), lambda i, me: (0, 0))] * count,
            out_specs=pl.BlockSpec((size, depth), lambda i, me: (i, 0)),
        ),
        out_shape=jax.ShapeDtypeStruct((width, depth), bf16),
        name="move",
    )(me, first, second, h, w, *pairs, *grads)


def swap(value, which):
    count = lax.axis_size("replica")
    branches = [
        functools.partial(
            lambda x, mask: lax.ppermute(x, "replica", [(s, s ^ mask) for s in range(count)]),
            mask=mask,
        )
        for mask in range(1, count)
    ]
    return lax.switch(which - 1, branches, value)


def shift(value, step):
    count = lax.axis_size("tensor")
    return lax.ppermute(value, "tensor", [(s, (s + step) % count) for s in range(count)])


def spread(value):
    count = lax.axis_size("tensor")
    return [value] + [shift(value, k) for k in range(1, count)]


def per_device(weights, hidden, out_grad, factor_start, matching):
    count = lax.axis_size("tensor")
    me = lax.axis_index("tensor").astype(jnp.int32).reshape(1)
    w, h, g = weights[0], hidden[0], out_grad[0]
    steps, rank, width = factor_start.shape
    tokens = h.shape[0] // steps

    grads = [g]
    for _ in range(1, count):
        grads.append(shift(grads[-1], 1))

    messages = project(me, factor_start.reshape(steps * rank, width), h, w, count, rank, tokens)
    arrived = [messages[0]] + [shift(messages[k], k) for k in range(1, count)]
    mine, left = left_products(g, arrived, tokens)
    ortho0, left = ortho_first(me, left, spread(differ(mine, swap(mine, matching[0]))))
    diff = (left.astype(f32) - swap(left, matching[1]).astype(f32)).astype(bf16)
    ortho1 = ortho_second(me, spread(diff))

    right0 = right_first(me, ortho0, h, w, grads, tokens)
    other0 = swap(right0, matching[0])
    right1 = right_second(me, ortho1, ortho0, h, w, right0, other0, grads, tokens)
    other1 = swap(right1, matching[1])
    return move(me, ortho0, ortho1, h, w, (right0, other0, right1, other1), grads, tokens)[None]


def solution(mesh):
    return jax.shard_map(
        per_device,
        mesh=mesh,
        in_specs=(
            P("replica", "tensor", None),
            P("replica", None, "tensor"),
            P("replica", None, "tensor"),
            P(None, None, "tensor"),
            P(),
        ),
        out_specs=P("replica", "tensor", None),
        check_vma=False,
    )
```

```python
import functools

import jax
import jax.numpy as jnp
from jax import lax
from jax.experimental import pallas as pl
from jax.experimental.pallas import tpu as pltpu
from jax.sharding import PartitionSpec as P

learn_rate = 0.1
momentum_decay = 0.9
older_share = learn_rate * (1.0 + momentum_decay)
bf16 = jnp.bfloat16
f32 = jnp.float32

VMEM = pl.BlockSpec(memory_space=pltpu.VMEM)
SMEM = pl.BlockSpec(memory_space=pltpu.SMEM)
HBM = pl.BlockSpec(memory_space=pltpu.HBM)
room = pltpu.CompilerParams(vmem_limit_bytes=28 * 2**20)


def dot(a, b, contract, precision=None):
    return lax.dot_general(
        a, b, (((contract[0],), (contract[1],)), ((), ())),
        precision=precision, preferred_element_type=f32,
    )


def exact(a, b, contract):
    return dot(a, b, contract, lax.Precision.HIGHEST)


def columns_of(place, width):
    return pl.ds(pl.multiple_of(place * width, width), width)


def write_pieces(out, parts, seen):
    at = 0
    for part in parts:
        out[:, at : at + part.shape[1]] = part
        at += part.shape[1]
    out[:, at:] = seen


def project_kernel(count, tokens, me_ref, f_hbm, h_hbm, w_hbm, kept, sent, w, h, f, total, sems):
    rank = kept.shape[0]
    span = w.shape[1] // count
    chunks = 4
    size = w.shape[0] // chunks
    first = pltpu.make_async_copy(f_hbm, f, sems.at[chunks])
    first.start()
    copies = []
    for i in range(chunks):
        at = pl.ds(i * size, size)
        copies.append(pltpu.make_async_copy(w_hbm.at[at], w.at[at], sems.at[i]))
        copies[-1].start()
    last = pltpu.make_async_copy(h_hbm, h, sems.at[chunks + 1])
    last.start()
    first.wait()
    for i in range(chunks):
        copies[i].wait()
        part = dot(f[:, i * size : (i + 1) * size], w[i * size : (i + 1) * size, :], (1, 0))
        total[...] = part if i == 0 else total[...] + part
    last.wait()
    both = dot(f[...], h[...], (1, 1)).astype(bf16)
    seen = jnp.concatenate(
        [both[:rank, :tokens], both[rank:, :tokens], both[rank:, tokens:]], 1
    )
    for out, start in ((kept, 0), (sent, 1)):
        parts = []
        for r in range(start, count, 2):
            part = total[:, columns_of(me_ref[0] ^ r, span)].astype(bf16)
            parts += [part[:rank], part[rank:]]
        write_pieces(out, parts, seen)


def project(me, factors, h, w, count, rank, tokens):
    _, depth = w.shape
    span = depth // count
    length = count * span + 3 * tokens
    message = jax.ShapeDtypeStruct((rank, length), bf16)
    return pl.pallas_call(
        functools.partial(project_kernel, count, tokens),
        in_specs=[SMEM, HBM, HBM, HBM],
        out_specs=[VMEM] * 2,
        out_shape=[message, message],
        scratch_shapes=[
            pltpu.VMEM(w.shape, bf16),
            pltpu.VMEM(h.shape, bf16),
            pltpu.VMEM(factors.shape, bf16),
            pltpu.VMEM((2 * rank, depth), f32),
            pltpu.SemaphoreType.DMA((6,)),
        ],
        compiler_params=room,
        name="project",
    )(me, *(pltpu.with_memory_space_constraint(x, pltpu.HBM) for x in (factors, h, w)))


def halve(kept, arrived, tokens, span):
    rank, length = kept.shape
    pieces = (length - 3 * tokens) // (2 * span)
    message = jax.ShapeDtypeStruct((rank, pieces * span + 3 * tokens), bf16)

    def kernel(kept, arrived, keep, send):
        total = (kept[...].astype(f32) + arrived[...].astype(f32)).astype(bf16)
        for out, start in ((keep, 0), (send, 1)):
            parts = [total[:, 2 * span * r : 2 * span * (r + 1)] for r in range(start, pieces, 2)]
            write_pieces(out, parts, total[:, 2 * span * pieces :])

    return pl.pallas_call(
        kernel, out_shape=[message] * 2, in_specs=[VMEM] * 2, out_specs=[VMEM] * 2,
        compiler_params=room, name="halve",
    )(kept, arrived)


def left_kernel(count, tokens, g_ref, *refs):
    messages, (mine, left) = refs[:count], refs[count:]
    span = g_ref.shape[1]
    total = messages[0][...].astype(f32)
    for k in range(1, count):
        total = total + messages[k][...].astype(f32)
    seen = total[:, 2 * span :].astype(bf16)
    older = dot(seen[:, tokens : 2 * tokens], g_ref[:tokens, :], (1, 0))
    mine[:, :span] = (
        total[:, :span] - learn_rate * dot(seen[:, :tokens], g_ref[:tokens, :], (1, 0))
    ).astype(bf16)
    later = total[:, span : 2 * span] - learn_rate * older
    mine[:, span:] = later.astype(bf16)
    left[...] = later - learn_rate * (
        momentum_decay * older + dot(seen[:, 2 * tokens :], g_ref[tokens:, :], (1, 0))
    )


def left_products(g, messages, tokens):
    rank, span = messages[0].shape[0], g.shape[1]
    return pl.pallas_call(
        functools.partial(left_kernel, len(messages), tokens),
        out_shape=[
            jax.ShapeDtypeStruct((rank, 2 * span), bf16),
            jax.ShapeDtypeStruct((rank, span), f32),
        ],
        in_specs=[VMEM] * (1 + len(messages)),
        out_specs=[VMEM] * 2,
        compiler_params=room,
        name="left",
    )(g, *messages)


def differ_kernel(mine, other, out):
    _, length = mine.shape
    span = length // 2
    diff = (mine[:, :span].astype(f32) - other[:, :span].astype(f32)).astype(bf16)
    both = (mine[:, span:].astype(f32) + other[:, span:].astype(f32)).astype(bf16)
    out[:, :span] = diff
    out[:, span:] = dot(both, diff, (1, 1)).astype(bf16)


def differ(mine, other):
    rank, length = mine.shape
    return pl.pallas_call(
        differ_kernel,
        out_shape=jax.ShapeDtypeStruct((rank, length // 2 + rank), bf16),
        in_specs=[VMEM] * 2,
        out_specs=VMEM,
        compiler_params=room,
        name="differ",
    )(mine, other)


def inverse_factor(gram):
    size = gram.shape[0]
    work = gram
    rows = lax.broadcasted_iota(jnp.int32, (size, size), 0)
    columns = lax.broadcasted_iota(jnp.int32, (size, size), 1)
    scale = jnp.ones((size, size), f32)
    for k in range(size):
        pivot_row = work[k : k + 1, :]
        pivot = work[k : k + 1, k : k + 1]
        row = jnp.where(columns[:1] == k, 1.0, pivot_row) / pivot
        ratio = jnp.where(rows > k, work[:, k : k + 1], 0.0)
        kept = jnp.where((columns == k) & (rows > k), 0.0, work)
        work = kept - ratio * row
        scale = jnp.where(rows == k, pivot, scale)
    lower = jnp.where(rows > columns, work, jnp.where(rows == columns, 1.0, 0.0))
    return lower * lax.rsqrt(scale)


def ortho_first_kernel(count, me_ref, left_ref, *refs):
    messages, (ortho, out, whole) = refs[:count], refs[count:]
    rank, span = left_ref.shape
    edge = jnp.zeros((rank, rank), f32)
    for k in range(count):
        place = lax.rem(me_ref[0] + count - k, count)
        whole[:, columns_of(place, span)] = messages[k][:, :span]
        edge = edge + messages[k][:, span:].astype(f32)
    inverse = inverse_factor(dot(whole[...], whole[...], (1, 1)))
    near = exact(inverse, messages[0][:, :span].astype(f32), (1, 0)).astype(bf16)
    turned = exact(edge, inverse, (1, 1)).astype(bf16)
    out[...] = (left_ref[...] - 0.5 * dot(turned, near, (1, 0))).astype(bf16)
    ortho[...] = exact(inverse, whole[...].astype(f32), (1, 0)).astype(bf16)


def ortho_first(me, left, messages):
    count = len(messages)
    rank, span = left.shape
    return pl.pallas_call(
        functools.partial(ortho_first_kernel, count),
        out_shape=[
            jax.ShapeDtypeStruct((rank, span * count), bf16),
            jax.ShapeDtypeStruct((rank, span), bf16),
        ],
        in_specs=[SMEM] + [VMEM] * (1 + count),
        out_specs=[VMEM] * 2,
        scratch_shapes=[pltpu.VMEM((rank, span * count), bf16)],
        compiler_params=room,
        name="ortho_first",
    )(me, left, *messages)


def ortho_second_kernel(whole, ortho, inverse):
    inverse[...] = inverse_factor(dot(whole[...], whole[...], (1, 1)))
    ortho[...] = exact(inverse[...], whole[...].astype(f32), (1, 0)).astype(bf16)


def ortho_second(whole):
    rank = whole.shape[0]
    return pl.pallas_call(
        ortho_second_kernel,
        out_shape=[jax.ShapeDtypeStruct(whole.shape, bf16), jax.ShapeDtypeStruct((rank, rank), f32)],
        in_specs=[VMEM],
        out_specs=[VMEM] * 2,
        compiler_params=room,
        name="ortho_second",
    )(whole)


def right_first_kernel(count, me_ref, ortho, h, w, *refs):
    grads, (out,) = refs[:count], refs[count:]
    tokens = h.shape[0] // 2
    span = grads[0].shape[1]
    total = jnp.zeros((ortho.shape[0], tokens), f32)
    for k in range(count):
        place = lax.rem(me_ref[0] + count - k, count)
        total = total + dot(ortho[:, columns_of(place, span)], grads[k][...], (1, 1))
    seen = (learn_rate * total).astype(bf16)
    out[...] = (
        dot(ortho[...], w[...], (1, 1)) - dot(seen, h[:tokens, :], (1, 0))
    ).astype(bf16)


def right_first(me, ortho, h, w, grads):
    return pl.pallas_call(
        functools.partial(right_first_kernel, len(grads)),
        in_specs=[SMEM] + [VMEM] * (3 + len(grads)),
        out_specs=VMEM,
        out_shape=jax.ShapeDtypeStruct((ortho.shape[0], w.shape[0]), bf16),
        compiler_params=room,
        name="right_first",
    )(me, ortho, h, w, *grads)


def descend_kernel(count, size, me_ref, h, w_hbm, *refs):
    grads, (out, w, u, loads, stores) = refs[:count], refs[count:]
    tokens, span = grads[0].shape
    blocks = w.shape[0] // size

    def load(i):
        at = pl.ds(i * size, size)
        return pltpu.make_async_copy(w_hbm.at[at], w.at[at], loads.at[i])

    def store(i):
        at = pl.ds(i * size, size)
        return pltpu.make_async_copy(u.at[at], out.at[at], stores.at[i])

    for i in range(blocks):
        load(i).start()

    def body(i, _):
        rows = pl.ds(pl.multiple_of(i * size, size), size)
        turned = (older_share * h[:tokens, rows].astype(f32)).astype(bf16).T
        load(i).wait()
        for k in range(count):
            at = columns_of(lax.rem(me_ref[0] + count - k, count), span)
            u[rows, at] = (
                w[rows, at].astype(f32) - dot(turned, grads[k][...], (1, 0))
            ).astype(bf16)
        store(i).start()
        return 0

    lax.fori_loop(0, blocks, body, 0)
    for i in range(blocks):
        store(i).wait()


def descend(me, h, w, grads):
    size = min(256, w.shape[0])
    blocks = w.shape[0] // size
    return pl.pallas_call(
        functools.partial(descend_kernel, len(grads), size),
        in_specs=[SMEM, VMEM, HBM] + [VMEM] * len(grads),
        out_specs=HBM,
        out_shape=jax.ShapeDtypeStruct(w.shape, bf16),
        scratch_shapes=[pltpu.VMEM(w.shape, bf16)] * 2
        + [pltpu.SemaphoreType.DMA((blocks,))] * 2,
        compiler_params=room,
        name="descend",
    )(me, h, pltpu.with_memory_space_constraint(w, pltpu.HBM), *grads)


def right_second_kernel(count, me_ref, before, h, w, mine, other, *refs):
    messages, olds, news = (refs[j * count : (j + 1) * count] for j in range(3))
    out, whole = refs[3 * count :]
    tokens = h.shape[0] // 2
    span = messages[0].shape[1]
    older = newer = jnp.zeros((before.shape[0], tokens), f32)
    for k in range(count):
        place = lax.rem(me_ref[0] + count - k, count)
        whole[:, columns_of(place, span)] = messages[k][...]
        older = older + dot(messages[k][...], olds[k][...], (1, 1))
        newer = newer + dot(messages[k][...], news[k][...], (1, 1))
    older = (older_share * older).astype(bf16)
    newer = (learn_rate * newer).astype(bf16)
    turned = (0.5 * dot(whole[...], before[...], (1, 1))).astype(bf16)
    turn = (mine[...].astype(f32) - other[...].astype(f32)).astype(bf16)
    out[...] = (
        dot(whole[...], w[...], (1, 1))
        - dot(jnp.concatenate([older, newer], 1), h[...], (1, 0))
        - dot(turned, turn, (1, 0))
    ).astype(bf16)


def right_second(me, before, h, w, mine, other, messages, olds, news):
    rank, depth = before.shape
    return pl.pallas_call(
        functools.partial(right_second_kernel, len(messages)),
        in_specs=[SMEM] + [VMEM] * (5 + 3 * len(messages)),
        out_specs=[VMEM] * 2,
        out_shape=[
            jax.ShapeDtypeStruct((rank, w.shape[0]), bf16),
            jax.ShapeDtypeStruct((rank, depth), bf16),
        ],
        compiler_params=room,
        name="right_second",
    )(me, before, h, w, mine, other, *messages, *olds, *news)


def move_kernel(count, me_ref, first, second, inverse, u, h, a0, b0, a1, b1, *refs):
    grads, (out, turn, ortho, block, sems) = refs[:count], refs[count:]
    rank = first.shape[0]
    tokens = h.shape[0] // 2
    span = grads[0].shape[1]
    size = min(256, u.shape[0])
    turn[:rank, :] = (0.5 * (a0[...].astype(f32) - b0[...].astype(f32))).astype(bf16)
    turn[rank : 2 * rank, :] = (
        0.5 * exact(inverse[...], a1[...].astype(f32) - b1[...].astype(f32), (1, 0))
    ).astype(bf16)
    turn[2 * rank :, :] = (learn_rate * h[tokens:, :].astype(f32)).astype(bf16)
    ortho[:rank, :] = first[...]
    ortho[rank : 2 * rank, :] = second[...]
    for k in range(count):
        at = columns_of(lax.rem(me_ref[0] + count - k, count), span)
        ortho[2 * rank :, at] = grads[k][...]
    copies = []
    for i in range(u.shape[0] // size):
        rows = slice(i * size, (i + 1) * size)
        block[rows, :] = (
            u[rows, :].astype(f32) - dot(turn[:, rows].T, ortho[...], (1, 0))
        ).astype(bf16)
        at = pl.ds(i * size, size)
        copies.append(pltpu.make_async_copy(block.at[at], out.at[at], sems.at[i]))
        copies[-1].start()
    for copy in copies:
        copy.wait()


def move(me, first, second, inverse, u, h, pairs, grads):
    rank = first.shape[0]
    tokens = h.shape[0] // 2
    depth = 2 * rank + tokens
    blocks = u.shape[0] // min(256, u.shape[0])
    return pl.pallas_call(
        functools.partial(move_kernel, len(grads)),
        in_specs=[SMEM] + [VMEM] * (9 + len(grads)),
        out_specs=HBM,
        out_shape=jax.ShapeDtypeStruct(u.shape, bf16),
        scratch_shapes=[
            pltpu.VMEM((depth, u.shape[0]), bf16),
            pltpu.VMEM((depth, u.shape[1]), bf16),
            pltpu.VMEM(u.shape, bf16),
            pltpu.SemaphoreType.DMA((blocks,)),
        ],
        compiler_params=room,
        name="move",
    )(me, first, second, inverse, u, h, *pairs, *grads)


def swap(value, which, beside=None):
    count = lax.axis_size("replica")

    def branch(x, mask):
        arrived = lax.ppermute(x, "replica", [(s, s ^ mask) for s in range(count)])
        return arrived, (beside() if beside else ())

    branches = [functools.partial(branch, mask=mask) for mask in range(1, count)]
    arrived, extra = lax.switch(which - 1, branches, value)
    return (arrived, extra) if beside else arrived


def shift(value, step):
    count = lax.axis_size("tensor")
    return lax.ppermute(value, "tensor", [(s, (s + step) % count) for s in range(count)])


def across(value, bit):
    count = lax.axis_size("tensor")
    return lax.ppermute(value, "tensor", [(s, s ^ bit) for s in range(count)])


def spread(value):
    count = lax.axis_size("tensor")
    return [value] + [shift(value, k) for k in range(1, count)]


def after(value, *events):
    return lax.optimization_barrier((value, *events))[0]


def per_device(weights, hidden, out_grad, factor_start, matching):
    return both_steps(weights[0], hidden[0], out_grad[0], factor_start, matching)[None]


def both_steps(w, h, g, factor_start, matching):
    count = lax.axis_size("tensor")
    me = lax.axis_index("tensor").astype(jnp.int32).reshape(1)
    steps, rank, width = factor_start.shape
    tokens = g.shape[0] // steps
    span = g.shape[1]

    first, second = [g[:tokens]], [g[tokens:]]
    first.append(shift(first[0], 1))
    kept, sent = project(
        me, factor_start.reshape(steps * rank, width), h, w, count, rank, tokens
    )
    bit = 1
    while True:
        arrived = across(sent, bit)
        bit *= 2
        if bit == count:
            break
        kept, sent = halve(kept, arrived, tokens, span)
    mine, left = left_products(g, [kept, arrived], tokens)
    first.append(shift(after(first[1], mine), 1))
    second.append(shift(after(second[0], mine), 1))
    other = swap(mine, matching[0])
    message = differ(mine, other)
    messages = spread(message)
    ortho0, left = ortho_first(me, left, messages)
    for _ in range(3, count):
        first.append(shift(after(first[-1], messages[-1]), 1))
    second.append(shift(after(second[1], messages[-1]), 1))
    other = swap(left, matching[1])
    diff = (left.astype(f32) - other.astype(f32)).astype(bf16)
    pieces = spread(diff)
    right0 = right_first(me, after(ortho0, diff), h, w, first)
    for _ in range(3, count):
        second.append(shift(after(second[-1], diff), 1))
    other0, u = swap(right0, matching[0], lambda: descend(me, h, w, first))
    right1, whole = right_second(me, ortho0, h, w, right0, other0, pieces, first, second)
    other1, (ortho1, inverse1) = swap(right1, matching[1], lambda: ortho_second(whole))
    return move(me, ortho0, ortho1, inverse1, u, h, (right0, other0, right1, other1), second)


def solution(mesh):
    return jax.shard_map(
        per_device,
        mesh=mesh,
        in_specs=(
            P("replica", "tensor", None),
            P("replica", None, "tensor"),
            P("replica", None, "tensor"),
            P(None, None, "tensor"),
            P(),
        ),
        out_specs=P("replica", "tensor", None),
        check_vma=False,
    )
```

```python
import functools

import jax
import jax.numpy as jnp
from jax import lax
from jax.experimental import pallas as pl
from jax.experimental.pallas import tpu as pltpu
from jax.sharding import PartitionSpec as P


learn_rate = 0.1
momentum_decay = 0.9
older_share = learn_rate * (1.0 + momentum_decay)
bf16 = jnp.bfloat16
f32 = jnp.float32

VMEM = pl.BlockSpec(memory_space=pltpu.VMEM)
SMEM = pl.BlockSpec(memory_space=pltpu.SMEM)
HBM = pl.BlockSpec(memory_space=pltpu.HBM)
room = pltpu.CompilerParams(vmem_limit_bytes=28 * 2**20)


def dot(a, b, contract, precision=None):
    return lax.dot_general(
        a, b, (((contract[0],), (contract[1],)), ((), ())),
        precision=precision, preferred_element_type=f32,
    )


def exact(a, b, contract):
    return dot(a, b, contract, lax.Precision.HIGHEST)


def in_hbm(*values):
    return [pltpu.with_memory_space_constraint(v, pltpu.HBM) for v in values]


def loading(source, target, sems, size):
    copies = []
    for i in range(source.shape[0] // size):
        at = pl.ds(i * size, size)
        copies.append(pltpu.make_async_copy(source.at[at], target.at[at], sems.at[i]))
        copies[-1].start()
    return copies


def columns_of(place, width):
    return pl.ds(pl.multiple_of(place * width, width), width)


def write_pieces(out, parts, seen):
    at = 0
    for part in parts:
        out[:, at : at + part.shape[1]] = part
        at += part.shape[1]
    out[:, at:] = seen


def project_kernel(count, tokens, me_ref, f_hbm, h_hbm, w_hbm, kept, sent, w, h, f, total, sems):
    rank = kept.shape[0]
    span = w.shape[1] // count
    chunks = 4
    size = w.shape[0] // chunks
    first = pltpu.make_async_copy(f_hbm, f, sems.at[chunks])
    first.start()
    copies = []
    for i in range(chunks):
        at = pl.ds(i * size, size)
        copies.append(pltpu.make_async_copy(w_hbm.at[at], w.at[at], sems.at[i]))
        copies[-1].start()
    last = pltpu.make_async_copy(h_hbm, h, sems.at[chunks + 1])
    last.start()
    first.wait()
    for i in range(chunks):
        copies[i].wait()
        part = dot(f[:, i * size : (i + 1) * size], w[i * size : (i + 1) * size, :], (1, 0))
        total[...] = part if i == 0 else total[...] + part
    last.wait()
    both = dot(f[...], h[...], (1, 1)).astype(bf16)
    seen = jnp.concatenate(
        [both[:rank, :tokens], both[rank:, :tokens], both[rank:, tokens:]], 1
    )
    for out, start in ((kept, 0), (sent, 1)):
        parts = []
        for r in range(start, count, 2):
            part = total[:, columns_of(me_ref[0] ^ r, span)].astype(bf16)
            parts += [part[:rank], part[rank:]]
        write_pieces(out, parts, seen)


def project(me, factors, h, w, count, rank, tokens):
    _, depth = w.shape
    span = depth // count
    length = count * span + 3 * tokens
    message = jax.ShapeDtypeStruct((rank, length), bf16)
    return pl.pallas_call(
        functools.partial(project_kernel, count, tokens),
        in_specs=[SMEM, HBM, HBM, HBM],
        out_specs=[VMEM] * 2,
        out_shape=[message, message],
        scratch_shapes=[
            pltpu.VMEM(w.shape, bf16),
            pltpu.VMEM(h.shape, bf16),
            pltpu.VMEM(factors.shape, bf16),
            pltpu.VMEM((2 * rank, depth), f32),
            pltpu.SemaphoreType.DMA((6,)),
        ],
        compiler_params=room,
        name="project",
    )(me, *(pltpu.with_memory_space_constraint(x, pltpu.HBM) for x in (factors, h, w)))


def halve(kept, arrived, tokens, span):
    rank, length = kept.shape
    pieces = (length - 3 * tokens) // (2 * span)
    message = jax.ShapeDtypeStruct((rank, pieces * span + 3 * tokens), bf16)

    def kernel(kept, arrived, keep, send):
        total = (kept[...].astype(f32) + arrived[...].astype(f32)).astype(bf16)
        for out, start in ((keep, 0), (send, 1)):
            parts = [total[:, 2 * span * r : 2 * span * (r + 1)] for r in range(start, pieces, 2)]
            write_pieces(out, parts, total[:, 2 * span * pieces :])

    return pl.pallas_call(
        kernel, out_shape=[message] * 2, in_specs=[VMEM] * 2, out_specs=[VMEM] * 2,
        compiler_params=room, name="halve",
    )(kept, arrived)


def left_kernel(count, tokens, g_ref, *refs):
    messages, (mine, left) = refs[:count], refs[count:]
    span = g_ref.shape[1]
    total = messages[0][...].astype(f32)
    for k in range(1, count):
        total = total + messages[k][...].astype(f32)
    seen = total[:, 2 * span :].astype(bf16)
    older = dot(seen[:, tokens : 2 * tokens], g_ref[:tokens, :], (1, 0))
    mine[:, :span] = (
        total[:, :span] - learn_rate * dot(seen[:, :tokens], g_ref[:tokens, :], (1, 0))
    ).astype(bf16)
    later = total[:, span : 2 * span] - learn_rate * older
    mine[:, span:] = later.astype(bf16)
    left[...] = later - learn_rate * (
        momentum_decay * older + dot(seen[:, 2 * tokens :], g_ref[tokens:, :], (1, 0))
    )


def left_products(g, messages, tokens):
    rank, span = messages[0].shape[0], g.shape[1]
    return pl.pallas_call(
        functools.partial(left_kernel, len(messages), tokens),
        out_shape=[
            jax.ShapeDtypeStruct((rank, 2 * span), bf16),
            jax.ShapeDtypeStruct((rank, span), f32),
        ],
        in_specs=[VMEM] * (1 + len(messages)),
        out_specs=[VMEM] * 2,
        compiler_params=room,
        name="left",
    )(g, *messages)


def differ_kernel(mine, other, out):
    _, length = mine.shape
    span = length // 2
    diff = (mine[:, :span].astype(f32) - other[:, :span].astype(f32)).astype(bf16)
    both = (mine[:, span:].astype(f32) + other[:, span:].astype(f32)).astype(bf16)
    out[:, :span] = diff
    out[:, span:] = dot(both, diff, (1, 1)).astype(bf16)


def differ(mine, other):
    rank, length = mine.shape
    return pl.pallas_call(
        differ_kernel,
        out_shape=jax.ShapeDtypeStruct((rank, length // 2 + rank), bf16),
        in_specs=[VMEM] * 2,
        out_specs=VMEM,
        compiler_params=room,
        name="differ",
    )(mine, other)


def differ_later_kernel(mine, other, g_ref, out):
    span = mine.shape[1]
    diff = (mine[...].astype(f32) - other[...].astype(f32)).astype(bf16)
    out[:, :span] = diff
    out[:, span:] = dot(diff, g_ref[...], (1, 1)).astype(bf16)


def differ_later(mine, other, g):
    rank, span = mine.shape
    return pl.pallas_call(
        differ_later_kernel,
        out_shape=jax.ShapeDtypeStruct((rank, span + g.shape[0]), bf16),
        in_specs=[VMEM] * 3,
        out_specs=VMEM,
        compiler_params=room,
        name="differ_later",
    )(mine, other, g)


def inverse_factor(gram):
    size = gram.shape[0]
    high = 8
    tiles = [gram[high * t : high * (t + 1), :] for t in range(size // high)]
    columns = lax.broadcasted_iota(jnp.int32, (high, size), 1)
    rows = lax.broadcasted_iota(jnp.int32, (high, size), 0)
    scales = []
    for own in range(size // high):
        below = range(own, size // high)
        ahead = [
            {t: jnp.broadcast_to(tiles[t][:, k : k + 1], (high, size)) for t in below}
            for k in range(high * own, high * (own + 1))
        ]
        scale = jnp.ones((high, size), f32)
        for j in range(high):
            k = high * own + j
            pivot = ahead[j][own][j : j + 1, :]
            share = 1.0 / pivot
            row = jnp.where(columns[:1] == k, 1.0, tiles[own][j : j + 1, :]) * share
            later = [ahead[m][own][j : j + 1, :] * share for m in range(high)]
            for t in below:
                ratio = jnp.where(rows > j, ahead[j][t], 0.0) if t == own else ahead[j][t]
                drop = (columns == k) & (rows > j) if t == own else columns == k
                tiles[t] = jnp.where(drop, 0.0, tiles[t]) - ratio * row
                for m in range(j + 1, high):
                    ahead[m][t] = ahead[m][t] - ratio * later[m]
            scale = jnp.where(rows == j, pivot, scale)
        scales.append(scale)
    out = []
    for t in range(size // high):
        place = rows + high * t
        lower = jnp.where(place > columns, tiles[t], jnp.where(place == columns, 1.0, 0.0))
        out.append(lower * lax.rsqrt(scales[t]))
    return jnp.concatenate(out, 0)


def ortho_first_kernel(count, me_ref, left_ref, *refs):
    messages, (ortho, out, whole) = refs[:count], refs[count:]
    rank, span = left_ref.shape
    edge = jnp.zeros((rank, rank), f32)
    for k in range(count):
        place = me_ref[0] ^ k
        whole[:, columns_of(place, span)] = messages[k][:, :span]
        edge = edge + messages[k][:, span:].astype(f32)
    inverse = inverse_factor(dot(whole[...], whole[...], (1, 1)))
    near = exact(inverse, messages[0][:, :span].astype(f32), (1, 0)).astype(bf16)
    turned = exact(edge, inverse, (1, 1)).astype(bf16)
    out[...] = (left_ref[...] - 0.5 * dot(turned, near, (1, 0))).astype(bf16)
    ortho[...] = exact(inverse, whole[...].astype(f32), (1, 0)).astype(bf16)


def ortho_first(me, left, messages):
    count = len(messages)
    rank, span = left.shape
    return pl.pallas_call(
        functools.partial(ortho_first_kernel, count),
        out_shape=[
            jax.ShapeDtypeStruct((rank, span * count), bf16),
            jax.ShapeDtypeStruct((rank, span), bf16),
        ],
        in_specs=[SMEM] + [VMEM] * (1 + count),
        out_specs=[VMEM] * 2,
        scratch_shapes=[pltpu.VMEM((rank, span * count), bf16)],
        compiler_params=room,
        name="ortho_first",
    )(me, left, *messages)


def inverse_factor_loop(work, scales):
    size, width = work.shape
    high = 8
    columns = lax.broadcasted_iota(jnp.int32, (high, width), 1)
    rows = lax.broadcasted_iota(jnp.int32, (high, width), 0)

    def body(own, _):
        base = own * high
        tiles = [work[high * t : high * (t + 1), :] for t in range(size // high)]
        tiles.append(work[pl.ds(pl.multiple_of(base, high), high), :])
        starts = [high * t for t in range(size // high)] + [base]
        turned = [pltpu.roll(tile, width - base, 1) for tile in tiles]
        ahead = [
            [jnp.broadcast_to(tile[:, j : j + 1], (high, width)) for tile in turned]
            for j in range(high)
        ]
        scale = jnp.ones((high, width), f32)
        for j in range(high):
            pivot = ahead[j][-1][j : j + 1, :]
            share = 1.0 / pivot
            row = jnp.where(columns[:1] == base + j, 1.0, tiles[-1][j : j + 1, :]) * share
            later = [ahead[m][-1][j : j + 1, :] * share for m in range(high)]
            for t, start in enumerate(starts):
                below = rows > base + j - start
                ratio = jnp.where(below, ahead[j][t], 0.0)
                drop = (columns == base + j) & below
                tiles[t] = jnp.where(drop, 0.0, tiles[t]) - ratio * row
                for m in range(j + 1, high):
                    ahead[m][t] = ahead[m][t] - ratio * later[m]
            scale = jnp.where(rows == j, pivot, scale)
        for t in range(size // high):
            work[high * t : high * (t + 1), :] = tiles[t]
        scales[pl.ds(pl.multiple_of(base, high), high), :] = scale
        return 0

    lax.fori_loop(0, size // high, body, 0)
    across = lax.broadcasted_iota(jnp.int32, (size, size), 1)
    down = lax.broadcasted_iota(jnp.int32, (size, size), 0)
    lower = jnp.where(down > across, work[:, :size], jnp.where(down == across, 1.0, 0.0))
    return lower * lax.rsqrt(scales[:, :size])


def ortho_second_kernel(whole, ortho, inverse, work, scales):
    rank, depth = whole.shape
    work[...] = jnp.zeros_like(work)
    work[:, :rank] = dot(whole[...], whole[...], (1, 1))
    inverse[...] = inverse_factor_loop(work, scales)
    size = min(512, depth)

    def body(i, _):
        at = columns_of(i, size)
        ortho[:, at] = exact(inverse[...], whole[:, at].astype(f32), (1, 0)).astype(bf16)
        return 0

    lax.fori_loop(0, depth // size, body, 0)


def ortho_second(whole):
    rank = whole.shape[0]
    return pl.pallas_call(
        ortho_second_kernel,
        out_shape=[jax.ShapeDtypeStruct(whole.shape, bf16), jax.ShapeDtypeStruct((rank, rank), f32)],
        in_specs=[VMEM],
        out_specs=[VMEM] * 2,
        scratch_shapes=[pltpu.VMEM((rank, 2 * rank), f32)] * 2,
        compiler_params=room,
        name="ortho_second",
    )(whole)


def right_first_kernel(count, me_ref, ortho, h_hbm, w_hbm, *refs):
    grads, (out, h, w, h_sems, w_sems) = refs[:count], refs[count:]
    tokens, span = grads[0].shape
    half = w.shape[0] // 2
    (seeing,) = loading(h_hbm.at[pl.ds(0, tokens)], h, h_sems, tokens)
    copies = loading(w_hbm, w, w_sems, half)
    total = jnp.zeros((ortho.shape[0], tokens), f32)
    for k in range(count):
        total = total + dot(ortho[:, columns_of(me_ref[0] ^ k, span)], grads[k][...], (1, 1))
    seen = (learn_rate * total).astype(bf16)
    seeing.wait()
    for i in range(2):
        at = slice(i * half, (i + 1) * half)
        change = dot(seen, h[:, at], (1, 0))
        copies[i].wait()
        out[:, at] = (dot(ortho[...], w[at, :], (1, 1)) - change).astype(bf16)


def right_first(me, ortho, h, w, grads):
    return pl.pallas_call(
        functools.partial(right_first_kernel, len(grads)),
        in_specs=[SMEM, VMEM, HBM, HBM] + [VMEM] * len(grads),
        out_specs=VMEM,
        out_shape=jax.ShapeDtypeStruct((ortho.shape[0], w.shape[0]), bf16),
        scratch_shapes=[
            pltpu.VMEM((h.shape[0] // 2, h.shape[1]), bf16),
            pltpu.VMEM(w.shape, bf16),
            pltpu.SemaphoreType.DMA((1,)),
            pltpu.SemaphoreType.DMA((2,)),
        ],
        compiler_params=room,
        name="right_first",
    )(me, ortho, *in_hbm(h, w), *grads)


def turn_kernel(h, old, new):
    tokens = h.shape[0] // 2
    size = min(512, h.shape[1])
    for i in range(h.shape[1] // size):
        at = slice(i * size, (i + 1) * size)
        old[at, :] = (older_share * h[:tokens, at].astype(f32)).astype(bf16).T
        new[at, :] = (learn_rate * h[tokens:, at].astype(f32)).astype(bf16).T


def turn(h):
    tokens = h.shape[0] // 2
    return pl.pallas_call(
        turn_kernel,
        in_specs=[VMEM],
        out_specs=[VMEM] * 2,
        out_shape=[jax.ShapeDtypeStruct((h.shape[1], tokens), bf16)] * 2,
        compiler_params=room,
        name="turn",
    )(h)


def descend_kernel(count, size, me_ref, h_hbm, w_hbm, *refs):
    pieces, (out, h, u, grads, h_sems, loads, stores) = refs[:count], refs[count:]
    span = pieces[0].shape[1]
    blocks = u.shape[0] // size
    loading(h_hbm, h, h_sems, size)
    loading(w_hbm, u, loads, size)
    for k in range(count):
        grads[:, columns_of(me_ref[0] ^ k, span)] = pieces[k][...]

    def body(i, _):
        rows = pl.ds(pl.multiple_of(i * size, size), size)
        pltpu.make_async_copy(h_hbm.at[rows], h.at[rows], h_sems.at[i]).wait()
        change = dot(h[rows, :], grads[...], (1, 0))
        pltpu.make_async_copy(w_hbm.at[rows], u.at[rows], loads.at[i]).wait()
        u[rows, :] = (u[rows, :].astype(f32) - change).astype(bf16)
        pltpu.make_async_copy(u.at[rows], out.at[rows], stores.at[i]).start()
        return 0

    lax.fori_loop(0, blocks, body, 0)
    for i in range(blocks):
        at = pl.ds(i * size, size)
        pltpu.make_async_copy(u.at[at], out.at[at], stores.at[i]).wait()


def descend(me, turned, w, pieces):
    size = min(256, w.shape[0])
    blocks = w.shape[0] // size
    return pl.pallas_call(
        functools.partial(descend_kernel, len(pieces), size),
        in_specs=[SMEM, HBM, HBM] + [VMEM] * len(pieces),
        out_specs=HBM,
        out_shape=pltpu.HBM(w.shape, bf16),
        scratch_shapes=[
            pltpu.VMEM(turned.shape, bf16),
            pltpu.VMEM(w.shape, bf16),
            pltpu.VMEM((turned.shape[1], w.shape[1]), bf16),
            pltpu.SemaphoreType.DMA((blocks,)),
            pltpu.SemaphoreType.DMA((blocks,)),
            pltpu.SemaphoreType.DMA((blocks,)),
        ],
        compiler_params=room,
        name="descend",
    )(me, *in_hbm(turned, w), *pieces)


def descend_later_kernel(count, size, me_ref, h, u, *refs):
    pieces, (out, grads) = refs[:count], refs[count:]
    span = pieces[0].shape[1]
    for k in range(count):
        grads[:, columns_of(me_ref[0] ^ k, span)] = pieces[k][...]

    def body(i, _):
        rows = pl.ds(pl.multiple_of(i * size, size), size)
        out[rows, :] = (u[rows, :].astype(f32) - dot(h[rows, :], grads[...], (1, 0))).astype(bf16)
        return 0

    lax.fori_loop(0, u.shape[0] // size, body, 0)


def descend_later(me, turned, u, pieces):
    return pl.pallas_call(
        functools.partial(descend_later_kernel, len(pieces), min(256, u.shape[0])),
        in_specs=[SMEM] + [VMEM] * (2 + len(pieces)),
        out_specs=VMEM,
        out_shape=jax.ShapeDtypeStruct(u.shape, bf16),
        scratch_shapes=[pltpu.VMEM((turned.shape[1], u.shape[1]), bf16)],
        compiler_params=room,
        name="descend_later",
    )(me, turned, u, *pieces)


def right_second_kernel(count, me_ref, before, h_hbm, u_hbm, mine, other, *refs):
    messages, (out, whole, h, u, h_sems, sems) = refs[:count], refs[count:]
    rank, tokens = before.shape[0], h.shape[0]
    span = messages[0].shape[1] - tokens
    half = u.shape[0] // 2
    (seeing,) = loading(h_hbm.at[pl.ds(tokens, tokens)], h, h_sems, tokens)
    copies = loading(u_hbm, u, sems, half)
    newer = jnp.zeros((rank, tokens), f32)
    for k in range(count):
        whole[:, columns_of(me_ref[0] ^ k, span)] = messages[k][:, :span]
        newer = newer + messages[k][:, span:].astype(f32)
    newer = (learn_rate * newer).astype(bf16)
    turned = (0.5 * dot(whole[...], before[...], (1, 1))).astype(bf16)
    seeing.wait()
    for i in range(2):
        at = slice(i * half, (i + 1) * half)
        turn = (mine[:, at].astype(f32) - other[:, at].astype(f32)).astype(bf16)
        change = dot(turned, turn, (1, 0)) + dot(newer, h[:, at], (1, 0))
        copies[i].wait()
        out[:, at] = (dot(whole[...], u[at, :], (1, 1)) - change).astype(bf16)


def right_second(me, before, h, u, mine, other, messages):
    rank, depth = before.shape
    return pl.pallas_call(
        functools.partial(right_second_kernel, len(messages)),
        in_specs=[SMEM, VMEM, HBM, HBM] + [VMEM] * (2 + len(messages)),
        out_specs=[VMEM] * 2,
        out_shape=[
            jax.ShapeDtypeStruct((rank, u.shape[0]), bf16),
            jax.ShapeDtypeStruct((rank, depth), bf16),
        ],
        scratch_shapes=[
            pltpu.VMEM((h.shape[0] // 2, h.shape[1]), bf16),
            pltpu.VMEM(u.shape, bf16),
            pltpu.SemaphoreType.DMA((1,)),
            pltpu.SemaphoreType.DMA((2,)),
        ],
        compiler_params=room,
        name="right_second",
    )(me, before, *in_hbm(h, u), mine, other, *messages)


def move_kernel(first, second, inverse, u, a0, b0, a1, b1, out, turned, ortho, block, stores):
    rank = first.shape[0]
    size = min(512, u.shape[0])
    both = jnp.concatenate(
        [
            a0[...].astype(f32) - b0[...].astype(f32),
            exact(inverse[...], a1[...].astype(f32) - b1[...].astype(f32), (1, 0)),
        ],
        0,
    )
    turned[...] = (0.5 * both).astype(bf16).T
    ortho[:rank, :] = first[...]
    ortho[rank:, :] = second[...]

    def body(i, _):
        rows = pl.ds(pl.multiple_of(i * size, size), size)
        block[rows, :] = (
            u[rows, :].astype(f32) - dot(turned[rows, :], ortho[...], (1, 0))
        ).astype(bf16)
        pltpu.make_async_copy(block.at[rows], out.at[rows], stores.at[i]).start()
        return 0

    blocks = u.shape[0] // size
    lax.fori_loop(0, blocks, body, 0)
    for i in range(blocks):
        at = pl.ds(i * size, size)
        pltpu.make_async_copy(block.at[at], out.at[at], stores.at[i]).wait()


def move(first, second, inverse, u, pairs):
    rank = first.shape[0]
    blocks = u.shape[0] // min(512, u.shape[0])
    return pl.pallas_call(
        move_kernel,
        in_specs=[VMEM] * 8,
        out_specs=HBM,
        out_shape=pltpu.HBM(u.shape, bf16),
        scratch_shapes=[
            pltpu.VMEM((u.shape[0], 2 * rank), bf16),
            pltpu.VMEM((2 * rank, u.shape[1]), bf16),
            pltpu.VMEM(u.shape, bf16),
            pltpu.SemaphoreType.DMA((blocks,)),
        ],
        compiler_params=room,
        name="move",
    )(first, second, inverse, u, *pairs)


def swap(value, which, beside=None, then=lambda arrived, extra: arrived):
    count = lax.axis_size("replica")

    def branch(x, mask):
        arrived = lax.ppermute(x, "replica", [(s, s ^ mask) for s in range(count)])
        return then(arrived, beside() if beside else None)

    branches = [functools.partial(branch, mask=mask) for mask in range(1, count)]
    return lax.switch(which - 1, branches, value)


def across(value, bit):
    count = lax.axis_size("tensor")
    return lax.ppermute(value, "tensor", [(s, s ^ bit) for s in range(count)])


def spread(value):
    pieces = [value]
    for r in range(1, lax.axis_size("tensor")):
        low = r & -r
        pieces.append(across(pieces[r ^ low], low))
    return pieces


def after(value, *events):
    return lax.optimization_barrier((value, *events))[0]


def per_device(weights, hidden, out_grad, factor_start, matching):
    return both_steps(weights[0], hidden[0], out_grad[0], factor_start, matching)[None]


def both_steps(w, h, g, factor_start, matching):
    count = lax.axis_size("tensor")
    me = lax.axis_index("tensor").astype(jnp.int32).reshape(1)
    steps, rank, width = factor_start.shape
    tokens = g.shape[0] // steps
    span = g.shape[1]
    olds, news = {0: g[:tokens]}, {0: g[tokens:]}

    def gather(pieces, event, *indices):
        for r in indices:
            low = r & -r
            pieces[r] = across(after(pieces[r ^ low], event), low)

    odd = range(1, count, 2)
    even = range(2, count, 2)
    kept, sent = project(me, factor_start.reshape(steps * rank, width), h, w, count, rank, tokens)
    bit = 1
    while True:
        arrived = across(sent, bit)
        if bit == 1:
            old_turned, new_turned = turn(after(h, sent))
            gather(olds, arrived, 1)
        bit *= 2
        if bit == count:
            break
        kept, sent = halve(kept, arrived, tokens, span)
    mine, left = left_products(g, [kept, arrived], tokens)
    gather(olds, mine, *even)
    other = swap(mine, matching[0])
    message = differ(mine, other)
    messages = spread(message)
    ortho0, left = ortho_first(me, left, messages)
    gather(olds, left, *odd[1:])
    other = swap(left, matching[1])
    message = differ_later(left, other, news[0])
    pieces = spread(message)
    olds = [olds[r] for r in range(count)]
    right0 = right_first(me, after(ortho0, message), h, w, olds)
    gather(news, pieces[2], *even)
    gather(news, pieces[2], 1)
    other0, u = swap(
        after(right0, pieces[2]),
        matching[0],
        lambda: descend(me, old_turned, w, olds),
        lambda *both: both,
    )
    gather(news, other0, *odd[1:])
    right1, whole = right_second(me, ortho0, h, u, right0, other0, pieces)
    news = [news[r] for r in range(count)]

    other1, (second, u) = swap(
        right1,
        matching[1],
        lambda: (ortho_second(whole), descend_later(me, new_turned, u, news)),
        lambda *both: both,
    )
    return move(ortho0, *second, u, (right0, other0, right1, other1))


def solution(mesh):
    return jax.shard_map(
        per_device,
        mesh=mesh,
        in_specs=(
            P("replica", "tensor", None),
            P("replica", None, "tensor"),
            P("replica", None, "tensor"),
            P(None, None, "tensor"),
            P(),
        ),
        out_specs=P("replica", "tensor", None),
        check_vma=False,
    )
```

```python
import functools

import jax
import jax.numpy as jnp
from jax import lax
from jax.experimental import pallas as pl
from jax.experimental.pallas import tpu as pltpu
from jax.sharding import PartitionSpec as P


learn_rate = 0.1
momentum_decay = 0.9
older_share = learn_rate * (1.0 + momentum_decay)
bf16 = jnp.bfloat16
f32 = jnp.float32

VMEM = pl.BlockSpec(memory_space=pltpu.VMEM)
SMEM = pl.BlockSpec(memory_space=pltpu.SMEM)
HBM = pl.BlockSpec(memory_space=pltpu.HBM)
room = pltpu.CompilerParams(vmem_limit_bytes=28 * 2**20)


def dot(a, b, contract, precision=None):
    return lax.dot_general(
        a, b, (((contract[0],), (contract[1],)), ((), ())),
        precision=precision, preferred_element_type=f32,
    )


def exact(a, b, contract):
    return dot(a, b, contract, lax.Precision.HIGHEST)


def in_hbm(*values):
    return [pltpu.with_memory_space_constraint(v, pltpu.HBM) for v in values]


def loading(source, target, sems, size):
    copies = []
    for i in range(source.shape[0] // size):
        at = pl.ds(i * size, size)
        copies.append(pltpu.make_async_copy(source.at[at], target.at[at], sems.at[i]))
        copies[-1].start()
    return copies


def columns_of(place, width):
    return pl.ds(pl.multiple_of(place * width, width), width)


def write_pieces(out, parts, seen):
    at = 0
    for part in parts:
        out[:, at : at + part.shape[1]] = part
        at += part.shape[1]
    out[:, at:] = seen


def project_sent_kernel(count, tokens, me_ref, f_hbm, h_hbm, w_hbm, sent, w, h, f, sems):
    rank = sent.shape[0]
    span = w.shape[2]
    odd = range(1, count, 2)
    copies = [pltpu.make_async_copy(f_hbm, f, sems.at[0])]
    for i, r in enumerate(odd):
        source = w_hbm.at[:, columns_of(me_ref[0] ^ r, span)]
        copies.append(pltpu.make_async_copy(source, w.at[i], sems.at[i + 1]))
    copies.append(pltpu.make_async_copy(h_hbm, h, sems.at[len(odd) + 1]))
    for copy in copies:
        copy.start()
    copies[0].wait()
    parts = []
    for i in range(len(odd)):
        copies[i + 1].wait()
        part = dot(f[...], w[i], (1, 0)).astype(bf16)
        parts += [part[:rank], part[rank:]]
    copies[-1].wait()
    both = dot(f[...], h[...], (1, 1)).astype(bf16)
    seen = jnp.concatenate(
        [both[:rank, :tokens], both[rank:, :tokens], both[rank:, tokens:]], 1
    )
    write_pieces(sent, parts, seen)


def project_kept_kernel(count, me_ref, f_hbm, w_hbm, sent, kept, w, f, sems):
    rank = kept.shape[0]
    span = w.shape[2]
    even = range(0, count, 2)
    copies = [pltpu.make_async_copy(f_hbm, f, sems.at[0])]
    for i, r in enumerate(even):
        source = w_hbm.at[:, columns_of(me_ref[0] ^ r, span)]
        copies.append(pltpu.make_async_copy(source, w.at[i], sems.at[i + 1]))
    for copy in copies:
        copy.start()
    copies[0].wait()
    parts = []
    for i in range(len(even)):
        copies[i + 1].wait()
        part = dot(f[...], w[i], (1, 0)).astype(bf16)
        parts += [part[:rank], part[rank:]]
    write_pieces(kept, parts, sent[:, count * span :])


def project_sent(me, factors, h, w, count, rank, tokens):
    width, depth = w.shape
    span = depth // count
    return pl.pallas_call(
        functools.partial(project_sent_kernel, count, tokens),
        in_specs=[SMEM, HBM, HBM, HBM],
        out_specs=VMEM,
        out_shape=jax.ShapeDtypeStruct((rank, count * span + 3 * tokens), bf16),
        scratch_shapes=[
            pltpu.VMEM((count // 2, width, span), bf16),
            pltpu.VMEM(h.shape, bf16),
            pltpu.VMEM(factors.shape, bf16),
            pltpu.SemaphoreType.DMA((count // 2 + 2,)),
        ],
        compiler_params=room,
        name="project_sent",
    )(me, *in_hbm(factors, h, w))


def project_kept(me, factors, w, sent, count):
    width, depth = w.shape
    return pl.pallas_call(
        functools.partial(project_kept_kernel, count),
        in_specs=[SMEM, HBM, HBM, VMEM],
        out_specs=VMEM,
        out_shape=jax.ShapeDtypeStruct(sent.shape, bf16),
        scratch_shapes=[
            pltpu.VMEM((count // 2, width, depth // count), bf16),
            pltpu.VMEM(factors.shape, bf16),
            pltpu.SemaphoreType.DMA((count // 2 + 1,)),
        ],
        compiler_params=room,
        name="project_kept",
    )(me, *in_hbm(factors, w), sent)


def halve(kept, arrived, tokens, span):
    rank, length = kept.shape
    pieces = (length - 3 * tokens) // (2 * span)
    message = jax.ShapeDtypeStruct((rank, pieces * span + 3 * tokens), bf16)

    def kernel(kept, arrived, keep, send):
        total = (kept[...].astype(f32) + arrived[...].astype(f32)).astype(bf16)
        for out, start in ((keep, 0), (send, 1)):
            parts = [total[:, 2 * span * r : 2 * span * (r + 1)] for r in range(start, pieces, 2)]
            write_pieces(out, parts, total[:, 2 * span * pieces :])

    return pl.pallas_call(
        kernel, out_shape=[message] * 2, in_specs=[VMEM] * 2, out_specs=[VMEM] * 2,
        compiler_params=room, name="halve",
    )(kept, arrived)


def left_kernel(count, tokens, g_ref, *refs):
    messages, (mine, left) = refs[:count], refs[count:]
    span = g_ref.shape[1]
    total = messages[0][...].astype(f32)
    for k in range(1, count):
        total = total + messages[k][...].astype(f32)
    seen = total[:, 2 * span :].astype(bf16)
    older = dot(seen[:, tokens : 2 * tokens], g_ref[:tokens, :], (1, 0))
    mine[:, :span] = (
        total[:, :span] - learn_rate * dot(seen[:, :tokens], g_ref[:tokens, :], (1, 0))
    ).astype(bf16)
    later = total[:, span : 2 * span] - learn_rate * older
    mine[:, span:] = later.astype(bf16)
    left[...] = later - learn_rate * (
        momentum_decay * older + dot(seen[:, 2 * tokens :], g_ref[tokens:, :], (1, 0))
    )


def left_products(g, messages, tokens):
    rank, span = messages[0].shape[0], g.shape[1]
    return pl.pallas_call(
        functools.partial(left_kernel, len(messages), tokens),
        out_shape=[
            jax.ShapeDtypeStruct((rank, 2 * span), bf16),
            jax.ShapeDtypeStruct((rank, span), f32),
        ],
        in_specs=[VMEM] * (1 + len(messages)),
        out_specs=[VMEM] * 2,
        compiler_params=room,
        name="left",
    )(g, *messages)


def differ_kernel(mine, other, out):
    _, length = mine.shape
    span = length // 2
    diff = (mine[:, :span].astype(f32) - other[:, :span].astype(f32)).astype(bf16)
    both = (mine[:, span:].astype(f32) + other[:, span:].astype(f32)).astype(bf16)
    out[:, :span] = diff
    out[:, span:] = dot(both, diff, (1, 1)).astype(bf16)


def differ(mine, other):
    rank, length = mine.shape
    return pl.pallas_call(
        differ_kernel,
        out_shape=jax.ShapeDtypeStruct((rank, length // 2 + rank), bf16),
        in_specs=[VMEM] * 2,
        out_specs=VMEM,
        compiler_params=room,
        name="differ",
    )(mine, other)


def differ_later_kernel(mine, other, g_ref, out):
    span = mine.shape[1]
    diff = (mine[...].astype(f32) - other[...].astype(f32)).astype(bf16)
    out[:, :span] = diff
    out[:, span:] = dot(diff, g_ref[...], (1, 1)).astype(bf16)


def differ_later(mine, other, g):
    rank, span = mine.shape
    return pl.pallas_call(
        differ_later_kernel,
        out_shape=jax.ShapeDtypeStruct((rank, span + g.shape[0]), bf16),
        in_specs=[VMEM] * 3,
        out_specs=VMEM,
        compiler_params=room,
        name="differ_later",
    )(mine, other, g)


def inverse_factor(gram):
    size = gram.shape[0]
    high = 8
    tiles = [gram[high * t : high * (t + 1), :] for t in range(size // high)]
    columns = lax.broadcasted_iota(jnp.int32, (high, size), 1)
    rows = lax.broadcasted_iota(jnp.int32, (high, size), 0)
    scales = []
    for own in range(size // high):
        below = range(own, size // high)
        ahead = [
            {t: jnp.broadcast_to(tiles[t][:, k : k + 1], (high, size)) for t in below}
            for k in range(high * own, high * (own + 1))
        ]
        scale = jnp.ones((high, size), f32)
        for j in range(high):
            k = high * own + j
            pivot = ahead[j][own][j : j + 1, :]
            share = 1.0 / pivot
            row = jnp.where(columns[:1] == k, 1.0, tiles[own][j : j + 1, :]) * share
            later = [ahead[m][own][j : j + 1, :] * share for m in range(high)]
            for t in below:
                ratio = jnp.where(rows > j, ahead[j][t], 0.0) if t == own else ahead[j][t]
                drop = (columns == k) & (rows > j) if t == own else columns == k
                tiles[t] = jnp.where(drop, 0.0, tiles[t]) - ratio * row
                for m in range(j + 1, high):
                    ahead[m][t] = ahead[m][t] - ratio * later[m]
            scale = jnp.where(rows == j, pivot, scale)
        scales.append(scale)
    out = []
    for t in range(size // high):
        place = rows + high * t
        lower = jnp.where(place > columns, tiles[t], jnp.where(place == columns, 1.0, 0.0))
        out.append(lower * lax.rsqrt(scales[t]))
    return jnp.concatenate(out, 0)


def ortho_first_kernel(count, me_ref, left_ref, *refs):
    messages, (ortho, out, whole) = refs[:count], refs[count:]
    rank, span = left_ref.shape
    edge = jnp.zeros((rank, rank), f32)
    for k in range(count):
        place = me_ref[0] ^ k
        whole[:, columns_of(place, span)] = messages[k][:, :span]
        edge = edge + messages[k][:, span:].astype(f32)
    inverse = inverse_factor(dot(whole[...], whole[...], (1, 1)))
    near = exact(inverse, messages[0][:, :span].astype(f32), (1, 0)).astype(bf16)
    turned = exact(edge, inverse, (1, 1)).astype(bf16)
    out[...] = (left_ref[...] - 0.5 * dot(turned, near, (1, 0))).astype(bf16)
    ortho[...] = exact(inverse, whole[...].astype(f32), (1, 0)).astype(bf16)


def ortho_first(me, left, messages):
    count = len(messages)
    rank, span = left.shape
    return pl.pallas_call(
        functools.partial(ortho_first_kernel, count),
        out_shape=[
            jax.ShapeDtypeStruct((rank, span * count), bf16),
            jax.ShapeDtypeStruct((rank, span), bf16),
        ],
        in_specs=[SMEM] + [VMEM] * (1 + count),
        out_specs=[VMEM] * 2,
        scratch_shapes=[pltpu.VMEM((rank, span * count), bf16)],
        compiler_params=room,
        name="ortho_first",
    )(me, left, *messages)


def inverse_factor_loop(work, scales):
    size, width = work.shape
    high = 8
    columns = lax.broadcasted_iota(jnp.int32, (high, width), 1)
    rows = lax.broadcasted_iota(jnp.int32, (high, width), 0)

    def body(own, _):
        base = own * high
        tiles = [work[high * t : high * (t + 1), :] for t in range(size // high)]
        tiles.append(work[pl.ds(pl.multiple_of(base, high), high), :])
        starts = [high * t for t in range(size // high)] + [base]
        turned = [pltpu.roll(tile, width - base, 1) for tile in tiles]
        ahead = [
            [jnp.broadcast_to(tile[:, j : j + 1], (high, width)) for tile in turned]
            for j in range(high)
        ]
        scale = jnp.ones((high, width), f32)
        for j in range(high):
            pivot = ahead[j][-1][j : j + 1, :]
            share = 1.0 / pivot
            row = jnp.where(columns[:1] == base + j, 1.0, tiles[-1][j : j + 1, :]) * share
            later = [ahead[m][-1][j : j + 1, :] * share for m in range(high)]
            for t, start in enumerate(starts):
                below = rows > base + j - start
                ratio = jnp.where(below, ahead[j][t], 0.0)
                drop = (columns == base + j) & below
                tiles[t] = jnp.where(drop, 0.0, tiles[t]) - ratio * row
                for m in range(j + 1, high):
                    ahead[m][t] = ahead[m][t] - ratio * later[m]
            scale = jnp.where(rows == j, pivot, scale)
        for t in range(size // high):
            work[high * t : high * (t + 1), :] = tiles[t]
        scales[pl.ds(pl.multiple_of(base, high), high), :] = scale
        return 0

    lax.fori_loop(0, size // high, body, 0)
    across = lax.broadcasted_iota(jnp.int32, (size, size), 1)
    down = lax.broadcasted_iota(jnp.int32, (size, size), 0)
    lower = jnp.where(down > across, work[:, :size], jnp.where(down == across, 1.0, 0.0))
    return lower * lax.rsqrt(scales[:, :size])


def ortho_second_kernel(whole, ortho, inverse, work, scales):
    rank, depth = whole.shape
    work[...] = jnp.zeros_like(work)
    work[:, :rank] = dot(whole[...], whole[...], (1, 1))
    inverse[...] = inverse_factor_loop(work, scales)
    size = min(512, depth)

    def body(i, _):
        at = columns_of(i, size)
        ortho[:, at] = exact(inverse[...], whole[:, at].astype(f32), (1, 0)).astype(bf16)
        return 0

    lax.fori_loop(0, depth // size, body, 0)


def ortho_second(whole):
    rank = whole.shape[0]
    return pl.pallas_call(
        ortho_second_kernel,
        out_shape=[jax.ShapeDtypeStruct(whole.shape, bf16), jax.ShapeDtypeStruct((rank, rank), f32)],
        in_specs=[VMEM],
        out_specs=[VMEM] * 2,
        scratch_shapes=[pltpu.VMEM((rank, 2 * rank), f32)] * 2,
        compiler_params=room,
        name="ortho_second",
    )(whole)


def right_first_kernel(count, me_ref, ortho, h_hbm, w_hbm, *refs):
    grads, (out, h, w, h_sems, w_sems) = refs[:count], refs[count:]
    tokens, span = grads[0].shape
    half = w.shape[0] // 2
    (seeing,) = loading(h_hbm.at[pl.ds(0, tokens)], h, h_sems, tokens)
    copies = loading(w_hbm, w, w_sems, half)
    total = jnp.zeros((ortho.shape[0], tokens), f32)
    for k in range(count):
        total = total + dot(ortho[:, columns_of(me_ref[0] ^ k, span)], grads[k][...], (1, 1))
    seen = (learn_rate * total).astype(bf16)
    seeing.wait()
    for i in range(2):
        at = slice(i * half, (i + 1) * half)
        change = dot(seen, h[:, at], (1, 0))
        copies[i].wait()
        out[:, at] = (dot(ortho[...], w[at, :], (1, 1)) - change).astype(bf16)


def right_first(me, ortho, h, w, grads):
    return pl.pallas_call(
        functools.partial(right_first_kernel, len(grads)),
        in_specs=[SMEM, VMEM, HBM, HBM] + [VMEM] * len(grads),
        out_specs=VMEM,
        out_shape=jax.ShapeDtypeStruct((ortho.shape[0], w.shape[0]), bf16),
        scratch_shapes=[
            pltpu.VMEM((h.shape[0] // 2, h.shape[1]), bf16),
            pltpu.VMEM(w.shape, bf16),
            pltpu.SemaphoreType.DMA((1,)),
            pltpu.SemaphoreType.DMA((2,)),
        ],
        compiler_params=room,
        name="right_first",
    )(me, ortho, *in_hbm(h, w), *grads)


def turn_kernel(h, old, new):
    tokens = h.shape[0] // 2
    size = min(512, h.shape[1])
    for i in range(h.shape[1] // size):
        at = slice(i * size, (i + 1) * size)
        old[at, :] = (older_share * h[:tokens, at].astype(f32)).astype(bf16).T
        new[at, :] = (learn_rate * h[tokens:, at].astype(f32)).astype(bf16).T


def turn(h):
    tokens = h.shape[0] // 2
    return pl.pallas_call(
        turn_kernel,
        in_specs=[VMEM],
        out_specs=[VMEM] * 2,
        out_shape=[jax.ShapeDtypeStruct((h.shape[1], tokens), bf16)] * 2,
        compiler_params=room,
        name="turn",
    )(h)


def descend_kernel(count, size, me_ref, h_hbm, w_hbm, *refs):
    pieces, (u, h, grads, h_sems, loads) = refs[:count], refs[count:]
    span = pieces[0].shape[1]
    blocks = u.shape[0] // size
    loading(h_hbm, h, h_sems, size)
    loading(w_hbm, u, loads, size)
    for k in range(count):
        grads[:, columns_of(me_ref[0] ^ k, span)] = pieces[k][...]

    def body(i, _):
        rows = pl.ds(pl.multiple_of(i * size, size), size)
        pltpu.make_async_copy(h_hbm.at[rows], h.at[rows], h_sems.at[i]).wait()
        change = dot(h[rows, :], grads[...], (1, 0))
        pltpu.make_async_copy(w_hbm.at[rows], u.at[rows], loads.at[i]).wait()
        u[rows, :] = (u[rows, :].astype(f32) - change).astype(bf16)
        return 0

    lax.fori_loop(0, blocks, body, 0)


def descend(me, turned, w, pieces):
    size = min(256, w.shape[0])
    blocks = w.shape[0] // size
    return pl.pallas_call(
        functools.partial(descend_kernel, len(pieces), size),
        in_specs=[SMEM, HBM, HBM] + [VMEM] * len(pieces),
        out_specs=VMEM,
        out_shape=pltpu.VMEM(w.shape, bf16),
        scratch_shapes=[
            pltpu.VMEM(turned.shape, bf16),
            pltpu.VMEM((turned.shape[1], w.shape[1]), bf16),
            pltpu.SemaphoreType.DMA((blocks,)),
            pltpu.SemaphoreType.DMA((blocks,)),
        ],
        compiler_params=room,
        name="descend",
    )(me, *in_hbm(turned, w), *pieces)


def descend_later_kernel(count, size, me_ref, h, u, *refs):
    pieces, (out, grads) = refs[:count], refs[count:]
    span = pieces[0].shape[1]
    for k in range(count):
        grads[:, columns_of(me_ref[0] ^ k, span)] = pieces[k][...]

    def body(i, _):
        rows = pl.ds(pl.multiple_of(i * size, size), size)
        out[rows, :] = (u[rows, :].astype(f32) - dot(h[rows, :], grads[...], (1, 0))).astype(bf16)
        return 0

    lax.fori_loop(0, u.shape[0] // size, body, 0)


def descend_later(me, turned, u, pieces):
    return pl.pallas_call(
        functools.partial(descend_later_kernel, len(pieces), min(256, u.shape[0])),
        in_specs=[SMEM] + [VMEM] * (2 + len(pieces)),
        out_specs=VMEM,
        out_shape=jax.ShapeDtypeStruct(u.shape, bf16),
        scratch_shapes=[pltpu.VMEM((turned.shape[1], u.shape[1]), bf16)],
        compiler_params=room,
        name="descend_later",
    )(me, turned, u, *pieces)


def right_second_kernel(count, me_ref, before, h_hbm, u, mine, other, *refs):
    messages, (out, whole, h, h_sems) = refs[:count], refs[count:]
    rank, tokens = before.shape[0], h.shape[0]
    span = messages[0].shape[1] - tokens
    (seeing,) = loading(h_hbm.at[pl.ds(tokens, tokens)], h, h_sems, tokens)
    newer = jnp.zeros((rank, tokens), f32)
    for k in range(count):
        whole[:, columns_of(me_ref[0] ^ k, span)] = messages[k][:, :span]
        newer = newer + messages[k][:, span:].astype(f32)
    newer = (learn_rate * newer).astype(bf16)
    turned = (0.5 * dot(whole[...], before[...], (1, 1))).astype(bf16)
    turn = (mine[...].astype(f32) - other[...].astype(f32)).astype(bf16)
    seeing.wait()
    out[...] = (
        dot(whole[...], u[...], (1, 1))
        - dot(turned, turn, (1, 0))
        - dot(newer, h[...], (1, 0))
    ).astype(bf16)


def right_second(me, before, h, u, mine, other, messages):
    rank, depth = before.shape
    return pl.pallas_call(
        functools.partial(right_second_kernel, len(messages)),
        in_specs=[SMEM, VMEM, HBM] + [VMEM] * (3 + len(messages)),
        out_specs=[VMEM] * 2,
        out_shape=[
            jax.ShapeDtypeStruct((rank, u.shape[0]), bf16),
            jax.ShapeDtypeStruct((rank, depth), bf16),
        ],
        scratch_shapes=[
            pltpu.VMEM((h.shape[0] // 2, h.shape[1]), bf16),
            pltpu.SemaphoreType.DMA((1,)),
        ],
        compiler_params=room,
        name="right_second",
    )(me, before, *in_hbm(h), u, mine, other, *messages)


def move_kernel(first, second, inverse, u, a0, b0, a1, b1, out, turned, ortho, block, stores):
    rank = first.shape[0]
    size = min(512, u.shape[0])
    both = jnp.concatenate(
        [
            a0[...].astype(f32) - b0[...].astype(f32),
            exact(inverse[...], a1[...].astype(f32) - b1[...].astype(f32), (1, 0)),
        ],
        0,
    )
    turned[...] = (0.5 * both).astype(bf16).T
    ortho[:rank, :] = first[...]
    ortho[rank:, :] = second[...]

    def body(i, _):
        rows = pl.ds(pl.multiple_of(i * size, size), size)
        block[rows, :] = (
            u[rows, :].astype(f32) - dot(turned[rows, :], ortho[...], (1, 0))
        ).astype(bf16)
        pltpu.make_async_copy(block.at[rows], out.at[rows], stores.at[i]).start()
        return 0

    blocks = u.shape[0] // size
    lax.fori_loop(0, blocks, body, 0)
    for i in range(blocks):
        at = pl.ds(i * size, size)
        pltpu.make_async_copy(block.at[at], out.at[at], stores.at[i]).wait()


def move(first, second, inverse, u, pairs):
    rank = first.shape[0]
    blocks = u.shape[0] // min(512, u.shape[0])
    return pl.pallas_call(
        move_kernel,
        in_specs=[VMEM] * 8,
        out_specs=HBM,
        out_shape=pltpu.HBM(u.shape, bf16),
        scratch_shapes=[
            pltpu.VMEM((u.shape[0], 2 * rank), bf16),
            pltpu.VMEM((2 * rank, u.shape[1]), bf16),
            pltpu.VMEM(u.shape, bf16),
            pltpu.SemaphoreType.DMA((blocks,)),
        ],
        compiler_params=room,
        name="move",
    )(first, second, inverse, u, *pairs)


def swap(value, which, beside=None, then=lambda arrived, extra: arrived):
    count = lax.axis_size("replica")

    def branch(x, mask):
        arrived = lax.ppermute(x, "replica", [(s, s ^ mask) for s in range(count)])
        return then(arrived, beside() if beside else None)

    branches = [functools.partial(branch, mask=mask) for mask in range(1, count)]
    return lax.switch(which - 1, branches, value)


def across(value, bit):
    count = lax.axis_size("tensor")
    return lax.ppermute(value, "tensor", [(s, s ^ bit) for s in range(count)])


def spread(value):
    pieces = [value]
    for r in range(1, lax.axis_size("tensor")):
        low = r & -r
        pieces.append(across(pieces[r ^ low], low))
    return pieces


def after(value, *events):
    return lax.optimization_barrier((value, *events))[0]


def per_device(weights, hidden, out_grad, factor_start, matching):
    return both_steps(weights[0], hidden[0], out_grad[0], factor_start, matching)[None]


def both_steps(w, h, g, factor_start, matching):
    count = lax.axis_size("tensor")
    me = lax.axis_index("tensor").astype(jnp.int32).reshape(1)
    steps, rank, width = factor_start.shape
    tokens = g.shape[0] // steps
    span = g.shape[1]
    olds, news = {0: g[:tokens]}, {0: g[tokens:]}

    def gather(pieces, event, *indices):
        for r in indices:
            low = r & -r
            pieces[r] = across(after(pieces[r ^ low], event), low)

    odd = range(1, count, 2)
    even = range(2, count, 2)
    factors = factor_start.reshape(steps * rank, width)
    sent = project_sent(me, factors, h, w, count, rank, tokens)
    kept = project_kept(me, factors, w, sent, count)
    bit = 1
    while True:
        arrived = across(sent, bit)
        if bit == 1:
            old_turned, new_turned = turn(after(h, sent))
            gather(olds, arrived, 1)
            gather(news, arrived, 1)
        bit *= 2
        if bit == count:
            break
        kept, sent = halve(kept, arrived, tokens, span)
    mine, left = left_products(g, [kept, arrived], tokens)
    gather(olds, mine, *even)
    other = swap(mine, matching[0])
    message = differ(mine, other)
    messages = spread(message)
    ortho0, left = ortho_first(me, left, messages)
    gather(olds, left, *odd[1:])
    gather(news, left, *even)
    other = swap(left, matching[1])
    message = differ_later(left, other, news[0])
    pieces = spread(message)
    olds = [olds[r] for r in range(count)]
    right0 = right_first(me, after(ortho0, message), h, w, olds)
    gather(news, pieces[2], *odd[1:])
    other0, u = swap(
        after(right0, pieces[2]),
        matching[0],
        lambda: descend(me, old_turned, w, olds),
        lambda *both: both,
    )
    right1, whole = right_second(me, ortho0, h, u, right0, other0, pieces)
    news = [news[r] for r in range(count)]

    other1, (second, u) = swap(
        right1,
        matching[1],
        lambda: (ortho_second(whole), descend_later(me, new_turned, u, news)),
        lambda *both: both,
    )
    return move(ortho0, *second, u, (right0, other0, right1, other1))


def solution(mesh):
    return jax.shard_map(
        per_device,
        mesh=mesh,
        in_specs=(
            P("replica", "tensor", None),
            P("replica", None, "tensor"),
            P("replica", None, "tensor"),
            P(None, None, "tensor"),
            P(),
        ),
        out_specs=P("replica", "tensor", None),
        check_vma=False,
    )
```
